32 devices in a mesh: ctx: 8 (over z, y), fsdp: 4 (over x, core).
Axes of the slice: x: 2, y: 2, z: 4, core: 2. Of those that a mesh axis runs over, the one named last changes fastest.
Arguments:
- tokens: bfloat16 [4, 1024, 768], P('fsdp', 'ctx'), may hold values from -6 to 6
- routes: int32 [4, 1024, 2], P('fsdp', 'ctx'), may hold values from 0 to 63, all different within a row; in each aligned block of 128 rows (0 to 127, 128 to 255, ..., all dimensions but the last counted through in order) at most 8 rows name the same one
- cotangent: bfloat16 [4, 1024, 768], P('fsdp', 'ctx'), may hold values from -6 to 6
- gains: bfloat16 [2, 768], P(None, ('ctx', 'fsdp')), may hold values from 0.25 to 1.75
- rel_bias: bfloat16 [384], P(('ctx', 'fsdp')), may hold values from -4 to 4
- attn_qkv: bfloat16 [2304, 768], P(('ctx', 'fsdp')), may hold values from -1.25 to 1.25
- attn_out: bfloat16 [768, 768], P(('ctx', 'fsdp')), may hold values from -0.875 to 0.875
- router: bfloat16 [768, 64], P(('ctx', 'fsdp')), may hold values from -0.875 to 0.875
- w_in: bfloat16 [64, 768, 3072], P('ctx', None, 'fsdp'), may hold values from -0.21875 to 0.21875
- w_out: bfloat16 [64, 3072, 768], P('ctx', 'fsdp'), may hold values from -0.109375 to 0.109375
Outputs:
- mixed: bfloat16 [4, 1024, 768], P('fsdp', 'ctx')
- d_tokens: float32 [4, 1024, 768], P('fsdp', 'ctx')
- d_gains: float32 [2, 768], P(None, ('ctx', 'fsdp'))
- d_rel_bias: float32 [384], P(('ctx', 'fsdp'))
- d_attn_qkv: float32 [2304, 768], P(('ctx', 'fsdp'))
- d_attn_out: float32 [768, 768], P(('ctx', 'fsdp'))
- d_router: float32 [768, 64], P(('ctx', 'fsdp'))
- d_w_in: float32 [64, 768, 3072], P('ctx', None, 'fsdp')
- d_w_out: float32 [64, 3072, 768], P('ctx', 'fsdp')
The draws below stay inside these ranges and needn't reach their ends.
Inputs may be any that keep to these rules, and one draw needn't show every extreme that they name: The two routes of a token name different experts. In each aligned block of 128 tokens of a sequence no expert is named more than 8 times, and some block names some expert exactly 8 times.
All inputs are finite; a program needn't handle non-finite values.
Results may differ from the reference program's by a relative error of at most 0.017.
The reference program's roundings to bfloat16 on the way count: a program that leaves them out, or rounds other values in their place, can miss the bound.
Values may be sent and summed in bfloat16 or wider, within the bound.
A program may use at most 320 MiB of HBM per device.

```python
import math
import jax
import jax.numpy as jnp
import numpy as np
from jax import lax

D = 768
H = 12
DH = 64
FF = 3072
E = 64
NB = 32
TOK_DEV = 128
CAP = 8
LEN = 1024
SEQS = 4
N_CTX = 8


def draw_attn_qkv(key, part):
    base = jax.random.truncated_normal(jax.random.fold_in(key, 11), -6.0, 6.0, (3 * D, D), jnp.float32)
    return (base / jnp.sqrt(jnp.float32(D))).astype(jnp.bfloat16)


def shard_levels(key, extent, shards, smallest, high):
    gain, own = 1.0, jax.random.fold_in(key, 6)
    for dim, parts in shards:
        draws = jnp.exp(jax.random.uniform(jax.random.fold_in(own, dim), (parts,), jnp.float32, smallest / len(shards), high / len(shards)))
        gain = gain * jnp.repeat(draws, extent[dim] // parts).reshape([-1 if axis == dim else 1 for axis in range(len(extent))])
    return gain


def shared_out(rng, own, number, rows, amount, top, most, lean):
    sequence = jax.random.permutation(rng, amount)
    packed, common = shares(amount, rows * top, most, lean, True), shares(amount, rows * top, most, lean, False)
    places = jnp.arange(amount)

    def named(sizes, rotation):
        used = int((sizes > 0).sum())
        fixed = max(1, used // 4)
        shifted = fixed + (places - fixed + rotation * (used - fixed)) % max(1, amount - fixed)
        return jnp.zeros((amount,), jnp.int32).at[sequence[jnp.where(places < fixed, places, shifted)]].set(jnp.asarray(sizes, jnp.int32))

    sizes = jnp.where(number % 4 == 0, named(packed, number // 4), named(common, number - number // 4 - 1))
    mixed = jax.random.permutation(jax.random.fold_in(own, 3), amount)
    donor, taker = mixed[0:amount // 2 * 2:2], mixed[1:amount // 2 * 2:2]
    slack = jnp.minimum(sizes[donor] - 1, most - sizes[taker]) // 2
    slack = jnp.where((donor == sequence[0]) | (taker == sequence[0]) | (sizes[taker] == 0), 0, jnp.maximum(slack, 0))
    shifted = jax.random.randint(jax.random.fold_in(own, 4), (amount // 2,), 0, 1 << 20) % (slack + 1)
    sizes = sizes.at[donor].add(-shifted).at[taker].add(shifted)
    items = jnp.searchsorted(jnp.cumsum(sizes), jnp.arange(rows * top), side="right").astype(jnp.int32)
    grid = items.reshape(top, rows).T
    grid = grid[jax.random.permutation(jax.random.fold_in(own, 1), rows)]
    rotation = jax.random.randint(jax.random.fold_in(own, 2), (rows, 1), 0, top)
    return jnp.take_along_axis(grid, (jnp.arange(top)[None, :] + rotation) % top, axis=1)


def shares(amount, total, most, lean, full):
    portions = [(1 << 20) // math.isqrt(standing ** lean) + 1 for standing in range(1, amount + 1)]
    largest = most if full else min(most, max(-(-total // amount), total * portions[0] // sum(portions)))
    least = 1 if total - largest >= amount - 1 else 0
    given, surplus = [largest] + [least] * (amount - 1), total - largest - least * (amount - 1)
    while surplus > 0:
        free = [i for i in range(1, amount) if given[i] < largest] or [i for i in range(1, amount) if given[i] < most]
        whole, left = sum([portions[i] for i in free]), surplus
        for i in free:
            addition = min(most - given[i], max(1, left * portions[i] // whole), surplus)
            given[i] = given[i] + addition
            surplus = surplus - addition
    return np.array(given)


def normal_values(key, shape, width, reach, cuts=(), kind=jnp.bfloat16):
    values = width * jax.random.normal(key, shape, jnp.float32)
    if cuts:
        values = values * shard_levels(key, shape, cuts, -0.22, 0.18)
    return jnp.clip(values, -reach, reach).astype(kind)


def setup_inputs(seed: int = 0) -> dict:
    arg_keys = jax.random.split(jax.random.key(seed), 11)
    tokens = normal_values(arg_keys[0], (SEQS, LEN, D), 1.0, 6.0, ((0, 4), (1, 8)))
    routes_keys = jax.random.split(jax.random.fold_in(arg_keys[1], 1), SEQS * LEN // TOK_DEV)
    routes_turns = jax.random.permutation(jax.random.fold_in(arg_keys[1], 3), SEQS * LEN // TOK_DEV)
    routes = jax.vmap(lambda own, number: shared_out(jax.random.fold_in(arg_keys[1], 2), own, number, TOK_DEV, E, 2, CAP, 2))(routes_keys, routes_turns).reshape((SEQS, LEN, 2))
    cotangent = normal_values(arg_keys[2], (SEQS, LEN, D), 1.0, 6.0, ((0, 4), (1, 8)))
    gains = jnp.clip(1.0 + 0.15 * jax.random.normal(arg_keys[3], (2, D), jnp.float32), 0.25, 1.75).astype(jnp.bfloat16)
    rel_bias = normal_values(arg_keys[4], (H * NB,), 1.0, 4.0, ((0, 32),))
    attn_qkv = draw_attn_qkv(jax.random.fold_in(arg_keys[10], 71), 0)
    attn_out = normal_values(arg_keys[6], (D, D), (D // 16) ** -0.5, 0.875, ((0, 32),))
    router = normal_values(arg_keys[7], (D, E), (D // 16) ** -0.5, 0.875, ((0, 32),))
    w_in = normal_values(arg_keys[8], (E, D, FF), D ** -0.5, 0.21875, ((0, 8), (2, 4)))
    w_out = normal_values(arg_keys[9], (E, FF, D), FF ** -0.5, 0.109375, ((0, 8), (1, 4)))
    return dict(tokens=tokens, routes=routes, cotangent=cotangent, gains=gains, rel_bias=rel_bias, attn_qkv=attn_qkv, attn_out=attn_out, router=router, w_in=w_in, w_out=w_out)


EPS = 1e-06
EDGES = (16, 23, 32, 45, 64, 91, 128, 181, 256, 362, 512, 724, 1024, 1448, 2048, 2896)
GELU_C = 0.7978845608028654
NEG = -1e+30

def bucket_of(offset):
    clipped = jnp.maximum(offset, 0)
    far = 15 + sum(((clipped >= edge).astype(jnp.int32) for edge in EDGES))
    return jnp.where(clipped < 16, clipped, far).astype(jnp.int32)

def norm_forward(values):
    inverse_norm = lax.rsqrt(lax.optimization_barrier(jnp.mean(values * values, axis=-1, keepdims=True)) + EPS)
    return (values * inverse_norm, inverse_norm)

def norm_backward(normalized_gradient, centered_rows, inverse_norm, gain_vector):
    centered_gradient = normalized_gradient * gain_vector
    gain_gradient = lax.optimization_barrier(jnp.sum(normalized_gradient * centered_rows, axis=0))
    value_gradients = inverse_norm * (centered_gradient - centered_rows * lax.optimization_barrier(jnp.mean(centered_gradient * centered_rows, axis=-1, keepdims=True)))
    return (value_gradients, gain_gradient)

def gelu_parts(pre):
    inner = GELU_C * (pre + 0.044715 * pre * pre * pre)
    tanh_v = jnp.tanh(inner)
    value = 0.5 * pre * (1.0 + tanh_v)
    slope = 0.5 * (1.0 + tanh_v) + 0.5 * pre * (1.0 - tanh_v * tanh_v) * GELU_C * (1.0 + 3.0 * 0.044715 * pre * pre)
    return (value, slope)

def block_scores(qpart, kpart, bias_table, qstart, kstart, scale):
    score = jnp.einsum('qhd,khd->hqk', qpart.astype(jnp.float32), kpart.astype(jnp.float32)) * scale
    offset = (qstart + jnp.arange(qpart.shape[0], dtype=jnp.int32))[:, None] - (kstart + jnp.arange(kpart.shape[0], dtype=jnp.int32))[None, :]
    bias_term = jnp.take(bias_table, bucket_of(offset), axis=1)
    return (jnp.where(offset[None] >= 0, score + bias_term, -jnp.inf), offset)

def reference(tokens, routes, cotangent, gains, rel_bias, attn_qkv, attn_out, router, w_in, w_out):
    single_float = jnp.float32
    bfloat_half = jnp.bfloat16
    rows = SEQS * LEN
    scale = 1.0 / math.sqrt(DH)
    qblk = math.gcd(LEN, 512)
    nqb = LEN // qblk
    input_rows = tokens.reshape(rows, D).astype(single_float)
    first_gain = gains[0].astype(single_float)
    second_gain = gains[1].astype(single_float)
    bias_table = rel_bias.astype(single_float).reshape(H, NB)
    w_qkv = attn_qkv.reshape(3, D, D)
    first_centered, first_inverse_norm = norm_forward(input_rows)
    first_normalized = (first_centered * first_gain).astype(bfloat_half)
    q = jnp.dot(first_normalized, w_qkv[0], preferred_element_type=single_float).astype(bfloat_half)
    k = jnp.dot(first_normalized, w_qkv[1], preferred_element_type=single_float).astype(bfloat_half)
    v = jnp.dot(first_normalized, w_qkv[2], preferred_element_type=single_float).astype(bfloat_half)
    heads_q = q.reshape(SEQS, LEN, H, DH)
    heads_k = k.reshape(SEQS, LEN, H, DH)
    heads_v = v.reshape(SEQS, LEN, H, DH)

    def forward_block(index):
        seq = (index // nqb).astype(jnp.int32)
        qstart = (index % nqb * qblk).astype(jnp.int32)
        qseq = lax.dynamic_index_in_dim(heads_q, seq, 0, keepdims=False)
        kseq = lax.dynamic_index_in_dim(heads_k, seq, 0, keepdims=False)
        vseq = lax.dynamic_index_in_dim(heads_v, seq, 0, keepdims=False)
        qpart = lax.dynamic_slice_in_dim(qseq, qstart, qblk, 0)

        def step(carry, kidx):
            run_max, total, acc = carry
            kstart = (kidx * qblk).astype(jnp.int32)
            kpart = lax.dynamic_slice_in_dim(kseq, kstart, qblk, 0)
            vpart = lax.dynamic_slice_in_dim(vseq, kstart, qblk, 0)
            score, _ = block_scores(qpart, kpart, bias_table, qstart, kstart, scale)
            newest = jnp.maximum(run_max, lax.optimization_barrier(jnp.max(score, axis=-1)))
            factor = jnp.exp(run_max - newest)
            weights = jnp.exp(score - newest[..., None])
            total = total * factor + lax.optimization_barrier(jnp.sum(weights, axis=-1))
            acc = acc * factor[..., None] + jnp.einsum('hqk,khd->hqd', weights.astype(bfloat_half).astype(single_float), vpart.astype(single_float))
            return ((newest, total, acc), None)
        init = (jnp.full((H, qblk), NEG, single_float), jnp.zeros((H, qblk), single_float), jnp.zeros((H, qblk, DH), single_float))
        (run_max, total, acc), _ = lax.scan(step, init, jnp.arange(nqb, dtype=jnp.int32))
        attended = (acc / total[..., None]).transpose(1, 0, 2).reshape(qblk, D).astype(bfloat_half)
        return (attended, run_max + jnp.log(total))
    attended_all, lse_all = lax.map(forward_block, jnp.arange(SEQS * nqb, dtype=jnp.int32))
    attended = attended_all.reshape(rows, D)
    lse_seq = lse_all.reshape(SEQS, nqb, H, qblk).transpose(0, 2, 1, 3).reshape(SEQS, H, LEN)
    first_hidden = input_rows + jnp.dot(attended, attn_out, preferred_element_type=single_float)
    second_centered, second_inverse_norm = norm_forward(first_hidden)
    second_normalized = (second_centered * second_gain).astype(bfloat_half)
    logits = jnp.dot(second_normalized, router, preferred_element_type=single_float)
    flat_routes = routes.reshape(rows, 2)
    chosen = jnp.take_along_axis(logits, flat_routes, axis=1)
    gate = jax.nn.softmax(chosen, axis=-1)
    nblk = SEQS * N_CTX
    assign = routes.reshape(nblk, 2 * TOK_DEV)
    member = (assign[..., None] == jnp.arange(E, dtype=jnp.int32)).astype(jnp.int32)
    slot = lax.optimization_barrier(jnp.sum((jnp.cumsum(member, axis=1) - member) * member, axis=-1)).astype(jnp.int32)
    doubled = jnp.repeat(second_normalized.reshape(nblk, TOK_DEV, D), 2, axis=1)
    block_ids = jnp.broadcast_to(jnp.arange(nblk, dtype=jnp.int32)[:, None], (nblk, 2 * TOK_DEV))
    buffer = jnp.zeros((nblk, E, CAP, D), bfloat_half).at[block_ids, assign, slot].set(doubled)
    expert_rows = buffer.transpose(1, 0, 2, 3).reshape(E, nblk * CAP, D)

    def expert_fwd(items):
        rows_e, win, wout = items
        hid, _ = gelu_parts(jnp.dot(rows_e, win, preferred_element_type=single_float))
        return jnp.dot(hid.astype(bfloat_half), wout, preferred_element_type=single_float).astype(bfloat_half)
    expert_out = lax.map(expert_fwd, (expert_rows, w_in, w_out))
    out_buffer = expert_out.reshape(E, nblk, CAP, D).transpose(1, 0, 2, 3)
    picked = out_buffer[block_ids, assign, slot].astype(single_float).reshape(rows, 2, D)
    mixed = (first_hidden + lax.optimization_barrier(jnp.sum(gate[..., None] * picked, axis=1))).astype(bfloat_half)
    dy = cotangent.reshape(rows, D).astype(single_float)
    dgate = lax.optimization_barrier(jnp.sum(dy[:, None, :] * picked, axis=-1))
    dchosen = gate * (dgate - lax.optimization_barrier(jnp.sum(gate * dgate, axis=-1, keepdims=True)))
    columns = (flat_routes[..., None] == jnp.arange(E, dtype=jnp.int32)).astype(single_float)
    dlogits = lax.optimization_barrier(jnp.sum(columns * dchosen[..., None], axis=1)).astype(bfloat_half)
    dpicked = (gate[..., None] * dy[:, None, :]).astype(bfloat_half).reshape(nblk, 2 * TOK_DEV, D)
    dbuffer = jnp.zeros((nblk, E, CAP, D), bfloat_half).at[block_ids, assign, slot].set(dpicked)
    dexpert_rows = dbuffer.transpose(1, 0, 2, 3).reshape(E, nblk * CAP, D)

    def expert_bwd(items):
        rows_e, drows, win, wout = items
        pre = jnp.dot(rows_e, win, preferred_element_type=single_float)
        hid, slope = gelu_parts(pre)
        dhid = jnp.dot(drows, wout.T, preferred_element_type=single_float)
        dpre = (dhid * slope).astype(bfloat_half)
        dwout = jnp.dot(hid.astype(bfloat_half).T, drows, preferred_element_type=single_float)
        dwin = jnp.dot(rows_e.T, dpre, preferred_element_type=single_float)
        dreturn = jnp.dot(dpre, win.T, preferred_element_type=single_float).astype(bfloat_half)
        return (dreturn, dwin, dwout)
    dreturn, d_w_in, d_w_out = lax.map(expert_bwd, (expert_rows, dexpert_rows, w_in, w_out))
    dreturn_buffer = dreturn.reshape(E, nblk, CAP, D).transpose(1, 0, 2, 3)
    dpicked_back = dreturn_buffer[block_ids, assign, slot].astype(single_float).reshape(rows, 2, D)
    second_normalized_gradient = lax.optimization_barrier(jnp.sum(dpicked_back, axis=1)) + jnp.dot(dlogits, router.T, preferred_element_type=single_float)
    d_router = jnp.dot(second_normalized.T, dlogits, preferred_element_type=single_float)
    second_norm_gradient, second_gain_gradient = norm_backward(second_normalized_gradient, second_centered, second_inverse_norm, second_gain)
    dh1 = dy + second_norm_gradient
    dh1_bf = dh1.astype(bfloat_half)
    d_attn_out = jnp.dot(attended.T, dh1_bf, preferred_element_type=single_float)
    dattended = jnp.dot(dh1_bf, attn_out.T, preferred_element_type=single_float).astype(bfloat_half)
    delta = lax.optimization_barrier(jnp.sum((dattended.astype(single_float) * attended.astype(single_float)).reshape(SEQS, LEN, H, DH), axis=-1)).transpose(0, 2, 1)
    heads_do = dattended.reshape(SEQS, LEN, H, DH)

    def backward_seq(seq):
        qseq = lax.dynamic_index_in_dim(heads_q, seq, 0, keepdims=False)
        kseq = lax.dynamic_index_in_dim(heads_k, seq, 0, keepdims=False)
        vseq = lax.dynamic_index_in_dim(heads_v, seq, 0, keepdims=False)
        doseq = lax.dynamic_index_in_dim(heads_do, seq, 0, keepdims=False)
        lse_here = lax.dynamic_index_in_dim(lse_seq, seq, 0, keepdims=False)
        delta_here = lax.dynamic_index_in_dim(delta, seq, 0, keepdims=False)

        def step(carry, qidx):
            dk, dv, dtable = carry
            qstart = (qidx * qblk).astype(jnp.int32)
            qpart = lax.dynamic_slice_in_dim(qseq, qstart, qblk, 0)
            dopart = lax.dynamic_slice_in_dim(doseq, qstart, qblk, 0)
            lse_part = lax.dynamic_slice_in_dim(lse_here, qstart, qblk, 1)
            delta_part = lax.dynamic_slice_in_dim(delta_here, qstart, qblk, 1)
            score, offset = block_scores(qpart, kseq, bias_table, qstart, jnp.int32(0), scale)
            weight = jnp.exp(score - lse_part[..., None])
            weight_bf = weight.astype(bfloat_half).astype(single_float)
            dweight = jnp.einsum('qhd,khd->hqk', dopart.astype(single_float), vseq.astype(single_float))
            score_gradient = weight * (dweight - delta_part[..., None])
            dscore_bf = score_gradient.astype(bfloat_half).astype(single_float)
            summed = jax.ops.segment_sum(score_gradient.transpose(1, 2, 0).reshape(qblk * LEN, H), bucket_of(offset).reshape(-1), num_segments=NB)
            dq_part = jnp.einsum('hqk,khd->qhd', dscore_bf, kseq.astype(single_float)) * scale
            dk = dk + jnp.einsum('hqk,qhd->khd', dscore_bf, qpart.astype(single_float)) * scale
            dv = dv + jnp.einsum('hqk,qhd->khd', weight_bf, dopart.astype(single_float))
            return ((dk, dv, dtable + summed.T), dq_part)
        init = (jnp.zeros((LEN, H, DH), single_float), jnp.zeros((LEN, H, DH), single_float), jnp.zeros((H, NB), single_float))
        (dk, dv, dtable), dq_parts = lax.scan(step, init, jnp.arange(nqb, dtype=jnp.int32))
        return (dq_parts.reshape(LEN, D).astype(bfloat_half), dk.reshape(LEN, D).astype(bfloat_half), dv.reshape(LEN, D).astype(bfloat_half), dtable)
    dq_all, dk_all, dv_all, dtables = lax.map(backward_seq, jnp.arange(SEQS, dtype=jnp.int32))
    grads_in = (dq_all.reshape(rows, D), dk_all.reshape(rows, D), dv_all.reshape(rows, D))
    d_attn_qkv = jnp.concatenate([jnp.dot(first_normalized.T, part, preferred_element_type=single_float) for part in grads_in], axis=0)
    first_normalized_gradient = jnp.dot(grads_in[0], w_qkv[0].T, preferred_element_type=single_float) + jnp.dot(grads_in[1], w_qkv[1].T, preferred_element_type=single_float) + jnp.dot(grads_in[2], w_qkv[2].T, preferred_element_type=single_float)
    first_norm_gradient, first_gain_gradient = norm_backward(first_normalized_gradient, first_centered, first_inverse_norm, first_gain)
    d_tokens = (dh1 + first_norm_gradient).reshape(SEQS, LEN, D)
    d_gains = jnp.stack([first_gain_gradient, second_gain_gradient])
    d_rel_bias = lax.optimization_barrier(jnp.sum(dtables, axis=0)).reshape(H * NB)
    return (mixed.reshape(SEQS, LEN, D), d_tokens, d_gains, d_rel_bias, d_attn_qkv, d_attn_out, d_router, d_w_in, d_w_out)
```

```python
import math

import jax
import jax.numpy as jnp
from jax import lax
from jax.sharding import PartitionSpec as P

D = 768
H = 12
DH = 64
E = 64
NB = 32
CAP = 8


EPS = 1e-06
EDGES = (16, 23, 32, 45, 64, 91, 128, 181, 256, 362, 512, 724, 1024, 1448, 2048, 2896)
GELU_C = 0.7978845608028654
NEG = -1e30


def bucket_of(offset):
    clipped = jnp.maximum(offset, 0)
    far = 15 + sum(((clipped >= edge).astype(jnp.int32) for edge in EDGES))
    return jnp.where(clipped < 16, clipped, far)


def norm_forward(values):
    inverse_norm = lax.rsqrt(jnp.mean(values * values, axis=-1, keepdims=True) + EPS)
    return (values * inverse_norm, inverse_norm)


def norm_backward(normalized_gradient, centered_rows, inverse_norm, gain_vector):
    centered_gradient = normalized_gradient * gain_vector
    gain_gradient = jnp.sum(normalized_gradient * centered_rows, axis=0)
    value_gradients = inverse_norm * (
        centered_gradient
        - centered_rows * jnp.mean(centered_gradient * centered_rows, axis=-1, keepdims=True)
    )
    return (value_gradients, gain_gradient)


def gelu_parts(pre):
    inner = GELU_C * (pre + 0.044715 * pre * pre * pre)
    tanh_v = jnp.tanh(inner)
    value = 0.5 * pre * (1.0 + tanh_v)
    slope = 0.5 * (1.0 + tanh_v) + 0.5 * pre * (1.0 - tanh_v * tanh_v) * GELU_C * (
        1.0 + 3.0 * 0.044715 * pre * pre
    )
    return (value, slope)


def block_terms(qheads, kpart, bias_table, qstart, kstart, scale):
    score = jnp.einsum("qhd,khd->hqk", qheads, kpart, preferred_element_type=jnp.float32) * scale
    offset = (qstart + jnp.arange(qheads.shape[0], dtype=jnp.int32))[:, None] - (
        kstart + jnp.arange(kpart.shape[0], dtype=jnp.int32)
    )[None, :]
    one_hot_mask = (
        bucket_of(offset)[None] == jnp.arange(NB, dtype=jnp.int32)[:, None, None]
    ).astype(jnp.bfloat16)
    bias_term = jnp.einsum(
        "fz,zmp->fmp", bias_table, one_hot_mask, preferred_element_type=jnp.float32
    )
    return (jnp.where(offset[None] >= 0, score + bias_term, -jnp.inf), one_hot_mask)


def shards(tokens, routes, cotangent, gains, rel_bias, attn_qkv, attn_out, router, w_in, w_out):
    single_float = jnp.float32
    bfloat_half = jnp.bfloat16
    tok = tokens.shape[1]
    n_ctx = lax.axis_size("ctx")
    seq_len = tok * n_ctx
    qstart = lax.axis_index("ctx") * tok
    qlast = qstart + tok - 1
    per_dev = w_in.shape[0]
    scale = 1.0 / math.sqrt(DH)
    kblk = math.gcd(seq_len, 512)
    axes = ("ctx", "fsdp")
    n_fsdp = lax.axis_size("fsdp")
    n_dev = n_ctx * n_fsdp
    qkv_rows, out_rows = attn_qkv.shape[0], attn_out.shape[0]
    tail_sizes = (router.size, gains.size, rel_bias.size)
    tail_used = sum(tail_sizes)
    tail_rows = -(-tail_used // D)
    head_rows = qkv_rows + out_rows
    pack_rows = -(-(head_rows + tail_rows) // 8) * 8
    tail = jnp.concatenate([router.reshape(-1), gains.reshape(-1), rel_bias.reshape(-1)])
    tail = jnp.pad(tail, (0, (pack_rows - head_rows) * D - tail_used))
    weights_pack = jnp.concatenate(
        [attn_qkv, attn_out, tail.reshape(pack_rows - head_rows, D)], axis=0
    )
    weights_all = lax.all_gather(weights_pack, axes, axis=0, tiled=False)
    qkv_full = weights_all[:, :qkv_rows].reshape(n_dev * qkv_rows, D)
    out_full = weights_all[:, qkv_rows:head_rows].reshape(n_dev * out_rows, D)
    tails = weights_all[:, head_rows:].reshape(n_dev, -1)
    cut_one = tail_sizes[0] + tail_sizes[1]
    router_full = tails[:, : tail_sizes[0]].reshape(D, E)
    gains_full = (
        tails[:, tail_sizes[0] : cut_one]
        .reshape(n_dev, 2, gains.shape[1])
        .transpose(1, 0, 2)
        .reshape(2, D)
    )
    bias_full = tails[:, cut_one:tail_used].reshape(H * NB)
    w_qkv = qkv_full.reshape(3, D, D)
    bias_table = bias_full.reshape(H, NB)
    first_gain = gains_full[0].astype(single_float)
    second_gain = gains_full[1].astype(single_float)
    input_rows = tokens.reshape(tok, D).astype(single_float)
    first_centered, first_inverse_norm = norm_forward(input_rows)
    first_normalized = (first_centered * first_gain).astype(bfloat_half)
    q = jnp.dot(first_normalized, w_qkv[0], preferred_element_type=single_float).astype(bfloat_half)
    k = jnp.dot(first_normalized, w_qkv[1], preferred_element_type=single_float).astype(bfloat_half)
    v = jnp.dot(first_normalized, w_qkv[2], preferred_element_type=single_float).astype(bfloat_half)
    keys_values = lax.all_gather(jnp.concatenate([k, v], axis=1), "ctx", axis=0, tiled=True)
    keys_all, values_all = keys_values[:, :D], keys_values[:, D:]
    qheads = q.reshape(tok, H, DH)
    kheads = keys_all.reshape(seq_len, H, DH)
    vheads = values_all.reshape(seq_len, H, DH)

    def keep(carry):
        return carry

    def forward_step(index, carry):
        kstart = index * kblk

        def forward_live(state):
            run_max, total, acc = state
            kpart = lax.dynamic_slice_in_dim(kheads, kstart, kblk, 0)
            vpart = lax.dynamic_slice_in_dim(vheads, kstart, kblk, 0)
            score, _ = block_terms(qheads, kpart, bias_table, qstart, kstart, scale)
            newest = jnp.maximum(run_max, jnp.max(score, axis=-1))
            factor = jnp.exp(run_max - newest)
            weights = jnp.exp(score - newest[..., None])
            total = total * factor + jnp.sum(weights, axis=-1)
            acc = acc * factor[..., None] + jnp.einsum(
                "hqk,khd->hqd",
                weights.astype(bfloat_half),
                vpart,
                preferred_element_type=single_float,
            )
            return (newest, total, acc)

        return lax.cond(kstart <= qlast, forward_live, keep, carry)

    init = (
        jnp.full((H, tok), NEG, single_float),
        jnp.zeros((H, tok), single_float),
        jnp.zeros((H, tok, DH), single_float),
    )
    run_max, total, acc = lax.fori_loop(0, seq_len // kblk, forward_step, init)
    lse = run_max + jnp.log(total)
    attended = (acc / total[..., None]).transpose(1, 0, 2).reshape(tok, D).astype(bfloat_half)
    first_hidden = input_rows + jnp.dot(attended, out_full, preferred_element_type=single_float)
    second_centered, second_inverse_norm = norm_forward(first_hidden)
    second_normalized = (second_centered * second_gain).astype(bfloat_half)
    logits = jnp.dot(second_normalized, router_full, preferred_element_type=single_float)
    expert_ids = jnp.arange(E, dtype=jnp.int32)
    chosen_mask = (routes.reshape(tok, 2)[:, :, None] == expert_ids).astype(single_float)
    chosen = jnp.sum(logits[:, None, :] * chosen_mask, axis=-1)
    gate = jax.nn.softmax(chosen, axis=-1)
    flat_routes = routes.reshape(2 * tok)
    member = (flat_routes[:, None] == expert_ids[None, :]).astype(jnp.int32)
    slot = jnp.sum((jnp.cumsum(member, axis=0) - member) * member, axis=1)
    target = flat_routes * CAP + slot
    table_disp = (target[:, None] == jnp.arange(E * CAP, dtype=jnp.int32)[None, :]).astype(
        bfloat_half
    )
    dy = cotangent.reshape(tok, D).astype(single_float)
    doubled = jnp.repeat(second_normalized, 2, axis=0)
    dpicked = (gate[:, :, None] * dy[:, None, :]).astype(bfloat_half).reshape(2 * tok, D)
    packed = (
        jnp.einsum(
            "ac,ad->cd",
            table_disp,
            jnp.concatenate([doubled, dpicked], axis=1),
            preferred_element_type=single_float,
        )
        .astype(bfloat_half)
        .reshape(n_ctx, per_dev, CAP, 2 * D)
    )
    received = lax.all_to_all(packed, "ctx", split_axis=0, concat_axis=0, tiled=True)
    rows_one = n_ctx * CAP
    received = received.transpose(1, 0, 2, 3).reshape(per_dev, rows_one, 2 * D)
    received_all = lax.all_gather(received, "fsdp", axis=0, tiled=False)
    received_all = received_all.transpose(1, 0, 2, 3).reshape(per_dev, n_fsdp * rows_one, 2 * D)
    buf, dbuf = received_all[:, :, :D], received_all[:, :, D:]
    hid, slope = gelu_parts(
        jnp.einsum("jcd,jdf->jcf", buf, w_in, preferred_element_type=single_float)
    )
    hid_bf = hid.astype(bfloat_half)
    dhid = jnp.einsum("jcd,jfd->jcf", dbuf, w_out, preferred_element_type=single_float)
    dpre = (dhid * slope).astype(bfloat_half)
    expert_part = jnp.einsum("jcf,jfd->jcd", hid_bf, w_out, preferred_element_type=single_float)
    dreturn_part = jnp.einsum("jcf,jdf->jcd", dpre, w_in, preferred_element_type=single_float)
    part = jnp.concatenate(
        [expert_part.astype(bfloat_half), dreturn_part.astype(bfloat_half)], axis=-1
    )
    part = part.reshape(per_dev, n_fsdp, rows_one, 2 * D).transpose(1, 0, 2, 3)
    part = part.reshape(n_fsdp * per_dev * rows_one, 2 * D)
    summed = lax.psum_scatter(part, "fsdp", scatter_dimension=0, tiled=True)
    d_w_out_mine = jnp.einsum("jcf,jcd->jfd", hid_bf, dbuf, preferred_element_type=single_float)
    d_w_in_mine = jnp.einsum("jcd,jcf->jdf", buf, dpre, preferred_element_type=single_float)
    summed = summed.reshape(per_dev, n_ctx, CAP, 2 * D).transpose(1, 0, 2, 3)
    returned = lax.all_to_all(summed, "ctx", split_axis=0, concat_axis=0, tiled=True)
    both = jnp.einsum(
        "ac,cd->ad", table_disp, returned.reshape(E * CAP, 2 * D), preferred_element_type=single_float
    ).reshape(tok, 2, 2 * D)
    picked = both[:, :, :D]
    mixed = (first_hidden + jnp.sum(gate[:, :, None] * picked, axis=1)).astype(bfloat_half)
    dgate = jnp.sum(dy[:, None, :] * picked, axis=-1)
    dchosen = gate * (dgate - jnp.sum(gate * dgate, axis=-1, keepdims=True))
    dlogits = jnp.sum(chosen_mask * dchosen[:, :, None], axis=1).astype(bfloat_half)
    second_normalized_gradient = jnp.sum(both[:, :, D:], axis=1)
    second_normalized_gradient = second_normalized_gradient + jnp.einsum(
        "te,de->td", dlogits, router_full, preferred_element_type=single_float
    )
    d_router_part = jnp.einsum(
        "td,te->de", second_normalized, dlogits, preferred_element_type=single_float
    )
    second_norm_gradient, second_gain_gradient = norm_backward(
        second_normalized_gradient, second_centered, second_inverse_norm, second_gain
    )
    dh1 = dy + second_norm_gradient
    dh1_bf = dh1.astype(bfloat_half)
    d_out_part = jnp.einsum("td,te->de", attended, dh1_bf, preferred_element_type=single_float)
    dattended = jnp.einsum(
        "te,de->td", dh1_bf, out_full, preferred_element_type=single_float
    ).astype(bfloat_half)
    do_heads = dattended.reshape(tok, H, DH)
    delta = jnp.sum(
        (dattended.astype(single_float) * attended.astype(single_float)).reshape(tok, H, DH),
        axis=-1,
    ).T

    def backward_step(index, carry):
        kstart = index * kblk

        def backward_live(state):
            dq, dk_all, dv_all, dtable = state
            kpart = lax.dynamic_slice_in_dim(kheads, kstart, kblk, 0)
            vpart = lax.dynamic_slice_in_dim(vheads, kstart, kblk, 0)
            score, one_hot_mask = block_terms(qheads, kpart, bias_table, qstart, kstart, scale)
            weight = jnp.exp(score - lse[..., None])
            weight_bf = weight.astype(bfloat_half)
            dweight = jnp.einsum(
                "qhd,khd->hqk", do_heads, vpart, preferred_element_type=single_float
            )
            score_gradient = weight * (dweight - delta[..., None])
            dscore_bf = score_gradient.astype(bfloat_half)
            dtable = dtable + jnp.einsum(
                "vwi,rwi->vr",
                score_gradient,
                one_hot_mask.astype(single_float),
                precision=lax.Precision.HIGHEST,
            )
            dq = (
                dq
                + jnp.einsum("hqk,khd->qhd", dscore_bf, kpart, preferred_element_type=single_float)
                * scale
            )
            dk_piece = (
                jnp.einsum("hqk,qhd->khd", dscore_bf, qheads, preferred_element_type=single_float)
                * scale
            )
            dv_piece = jnp.einsum(
                "hqk,qhd->khd", weight_bf, do_heads, preferred_element_type=single_float
            )
            dk_all = lax.dynamic_update_slice_in_dim(dk_all, dk_piece, kstart, 0)
            dv_all = lax.dynamic_update_slice_in_dim(dv_all, dv_piece, kstart, 0)
            return (dq, dk_all, dv_all, dtable)

        return lax.cond(kstart <= qlast, backward_live, keep, carry)

    init_back = (
        jnp.zeros((tok, H, DH), single_float),
        jnp.zeros((seq_len, H, DH), single_float),
        jnp.zeros((seq_len, H, DH), single_float),
        jnp.zeros((H, NB), single_float),
    )
    dq, dk_all, dv_all, dtable = lax.fori_loop(0, seq_len // kblk, backward_step, init_back)
    dkv = jnp.concatenate(
        [
            dk_all.reshape(seq_len, D).astype(bfloat_half),
            dv_all.reshape(seq_len, D).astype(bfloat_half),
        ],
        axis=1,
    )
    dkv_mine = lax.psum_scatter(dkv, "ctx", scatter_dimension=0, tiled=True)
    grads_in = (dq.reshape(tok, D).astype(bfloat_half), dkv_mine[:, :D], dkv_mine[:, D:])
    d_qkv_part = jnp.concatenate(
        [
            jnp.einsum("td,te->de", first_normalized, part, preferred_element_type=single_float)
            for part in grads_in
        ],
        axis=0,
    )
    first_normalized_gradient = jnp.einsum(
        "te,de->td", grads_in[0], w_qkv[0], preferred_element_type=single_float
    )
    first_normalized_gradient = first_normalized_gradient + jnp.einsum(
        "te,de->td", grads_in[1], w_qkv[1], preferred_element_type=single_float
    )
    first_normalized_gradient = first_normalized_gradient + jnp.einsum(
        "te,de->td", grads_in[2], w_qkv[2], preferred_element_type=single_float
    )
    first_norm_gradient, first_gain_gradient = norm_backward(
        first_normalized_gradient, first_centered, first_inverse_norm, first_gain
    )
    d_tokens = (dh1 + first_norm_gradient).reshape(1, tok, D)
    d_gains_part = jnp.stack([first_gain_gradient, second_gain_gradient])
    d_tail = jnp.concatenate(
        [
            d_router_part.reshape(n_dev, tail_sizes[0]),
            d_gains_part.reshape(2, n_dev, gains.shape[1])
            .transpose(1, 0, 2)
            .reshape(n_dev, tail_sizes[1]),
            dtable.reshape(n_dev, tail_sizes[2]),
        ],
        axis=1,
    )
    d_tail = jnp.pad(d_tail, ((0, 0), (0, (pack_rows - head_rows) * D - tail_used)))
    d_pack = jnp.concatenate(
        [
            d_qkv_part.reshape(n_dev, qkv_rows, D),
            d_out_part.reshape(n_dev, out_rows, D),
            d_tail.reshape(n_dev, pack_rows - head_rows, D),
        ],
        axis=1,
    )
    d_mine = lax.psum_scatter(d_pack, axes, scatter_dimension=0, tiled=False)
    d_qkv_mine, d_out_mine = d_mine[:qkv_rows], d_mine[qkv_rows:head_rows]
    tail_mine = d_mine[head_rows:].reshape(-1)
    d_router_mine = tail_mine[: tail_sizes[0]].reshape(router.shape)
    d_gains_mine = tail_mine[tail_sizes[0] : cut_one].reshape(gains.shape)
    d_bias_mine = tail_mine[cut_one:tail_used]
    return (
        mixed.reshape(1, tok, D),
        d_tokens,
        d_gains_mine,
        d_bias_mine,
        d_qkv_mine,
        d_out_mine,
        d_router_mine,
        d_w_in_mine,
        d_w_out_mine,
    )


def solution(mesh):
    return jax.shard_map(
        shards,
        mesh=mesh,
        in_specs=(
            P("fsdp", "ctx", None),
            P("fsdp", "ctx", None),
            P("fsdp", "ctx", None),
            P(None, ("ctx", "fsdp")),
            P(("ctx", "fsdp")),
            P(("ctx", "fsdp"), None),
            P(("ctx", "fsdp"), None),
            P(("ctx", "fsdp"), None),
            P("ctx", None, "fsdp"),
            P("ctx", "fsdp", None),
        ),
        out_specs=(
            P("fsdp", "ctx", None),
            P("fsdp", "ctx", None),
            P(None, ("ctx", "fsdp")),
            P(("ctx", "fsdp")),
            P(("ctx", "fsdp"), None),
            P(("ctx", "fsdp"), None),
            P(("ctx", "fsdp"), None),
            P("ctx", None, "fsdp"),
            P("ctx", "fsdp", None),
        ),
        check_vma=False,
    )
```
